128 devices in a mesh: dp: 16 (over x_hi, y, core), ind: 8 (over x_lo, z).
Axes of the slice: x: 4 (x_hi: 2, x_lo: 2; x = x_hi * 2 + x_lo), y: 4, z: 4, core: 2. Of those that a mesh axis runs over, the one named last changes fastest.
Arguments:
- x_points: float32 [3, 32768], P(None, 'dp'), may hold values from 0 to 1
- z_points: float32 [3, 16384], P(None, 'ind'), may hold values from 0 to 1
- length_scales: float32 [3], replicated, may hold values from 0.35 to 0.7
- dpsi_grad: float32 [16384, 16384], P('dp', 'ind'), may hold values from -0.625 to 0.625
- block_rows: int32 [16, 8, 3], P('dp', 'ind'), may hold values from 0 to 7, as said below
- block_cols: int32 [16, 8, 3], P('dp', 'ind'), may hold values from 0 to 7, as said below
- block_count: int32 [16, 8], P('dp', 'ind'), may hold values from 1 to 3, as said below
Outputs:
- dk_blocks: float32 [16, 8, 3, 256, 256], P('dp', 'ind')
- z_grad: float32 [3, 16384], P(None, 'ind')
- scale_grad: float32 [3], replicated
The draws below stay inside these ranges and needn't reach their ends.
Inputs may be any that keep to these rules, and one draw needn't show every extreme that they name: `block_rows`: within a tile the live slots lie in distinct row blocks, and the live slots of all tiles of one row group lie in at most 3 distinct row blocks; entries of unused slots carry no meaning. `block_cols`: entries of unused slots carry no meaning. `block_count`: some tile holds exactly 3 listed blocks in every draw.
All inputs are finite; a program needn't handle non-finite values.
Results may differ from the reference program's by a relative error of at most 0.0003.
Values sent between devices are 32-bit elements; how exact they have to be, the bound alone decides.
No kernel may reach another device: no remote copies, remote signals or barrier semaphores. Data moves between devices by JAX's collectives and lax.ppermute only.
A program may use at most 128 MiB of HBM per device.

```python
import math
import jax
import jax.numpy as jnp
from jax import lax

Q = 3
M = 16384
BS = 256
RB_DEV = 8
ROW_GROUPS = 16
COL_GROUPS = 8
CB_DEV = 8
CAP = 3
N = 32768


def pattern_parts(key):
    tiles_total = ROW_GROUPS * COL_GROUPS
    row_scores = jax.random.randint(jax.random.fold_in(key, 101), (ROW_GROUPS, RB_DEV), 0, 1 << 20)
    row_scores = row_scores * RB_DEV + jnp.arange(RB_DEV, dtype=jnp.int32)[None, :]
    active = jnp.argsort(row_scores, axis=1)[:, :CAP].astype(jnp.int32)
    slot_scores = jax.random.randint(jax.random.fold_in(key, 102), (ROW_GROUPS, COL_GROUPS, CAP), 0, 1 << 20)
    slot_scores = slot_scores * CAP + jnp.arange(CAP, dtype=jnp.int32)[None, None, :]
    order = jnp.argsort(slot_scores, axis=2).astype(jnp.int32)
    spread = jnp.broadcast_to(active[:, None, :], (ROW_GROUPS, COL_GROUPS, CAP))
    rows = jnp.take_along_axis(spread, order, axis=2).astype(jnp.int32)
    cols = jax.random.randint(jax.random.fold_in(key, 103), (ROW_GROUPS, COL_GROUPS, CAP), 0, CB_DEV).astype(jnp.int32)
    lowest = CAP // 2
    counts = jax.random.randint(jax.random.fold_in(key, 104), (tiles_total,), lowest, CAP + 1)
    full_tile = jax.random.randint(jax.random.fold_in(key, 105), (), 0, tiles_total)
    low_tile = (full_tile + 1 + jax.random.randint(jax.random.fold_in(key, 106), (), 0, tiles_total - 1)) % tiles_total
    tile_ids = jnp.arange(tiles_total, dtype=jnp.int32)
    counts = jnp.where(tile_ids == full_tile, CAP, counts)
    counts = jnp.where(tile_ids == low_tile, lowest, counts).astype(jnp.int32)
    return (rows, cols, counts.reshape(ROW_GROUPS, COL_GROUPS))


def draw_block_rows(key, part):
    return pattern_parts(key)[0]


def draw_block_cols(key, part):
    return pattern_parts(key)[1]


def draw_block_count(key, part):
    return pattern_parts(key)[2]


def shard_levels(rng, shape, cuts, smallest, high):
    gain, own = 1.0, jax.random.fold_in(rng, 6)
    for position, shards_of in cuts:
        draws = jnp.exp(jax.random.uniform(jax.random.fold_in(own, position), (shards_of,), jnp.float32, smallest / len(cuts), high / len(cuts)))
        gain = gain * jnp.repeat(draws, shape[position] // shards_of).reshape([-1 if axis == position else 1 for axis in range(len(shape))])
    return gain


def normal_values(rng, extent, scale, bound, split=(), kind=jnp.bfloat16):
    values = jax.random.normal(rng, extent, jnp.float32) * scale
    if len(split) > 0:
        values = shard_levels(rng, extent, split, -0.22, 0.18) * values
    return jnp.clip(values, min=-bound, max=bound).astype(kind)


def setup_inputs(seed: int = 0) -> dict:
    streams_of = jax.random.split(jax.random.key(seed), 8)
    return {
        "x_points": jnp.clip(1.0 * jax.random.uniform(streams_of[0], (Q, N), jnp.float32) ** shard_levels(streams_of[0], (Q, N), ((1, 16),), -0.2, 0.2), 0.0, 1.0),
        "z_points": jnp.clip(1.0 * jax.random.uniform(streams_of[1], (Q, M), jnp.float32) ** shard_levels(streams_of[1], (Q, M), ((1, 8),), -0.2, 0.2), 0.0, 1.0),
        "length_scales": jnp.clip(jnp.exp(jax.random.uniform(streams_of[2], (Q,), jnp.float32, math.log(0.35), math.log(0.7))), 0.35, 0.7),
        "dpsi_grad": normal_values(streams_of[3], (M, M), 0.1, 0.625, ((0, 16), (1, 8)), jnp.float32),
        "block_rows": draw_block_rows(jax.random.fold_in(streams_of[7], 71), 0),
        "block_cols": draw_block_cols(jax.random.fold_in(streams_of[7], 71), 0),
        "block_count": draw_block_count(jax.random.fold_in(streams_of[7], 71), 0),
    }


def wendland(x_rows, z_cols, length_scales):
    dist_sq = jnp.zeros((x_rows.shape[1], z_cols.shape[1]), x_rows.dtype)
    for dim_q in range(x_rows.shape[0]):
        offset = (x_rows[dim_q][:, None] - z_cols[dim_q][None, :]) / length_scales[dim_q]
        dist_sq = dist_sq + offset * offset
    radius = jnp.sqrt(dist_sq)
    remain = jnp.maximum(1.0 - radius, 0.0)
    remain_cube = remain * remain * remain
    return (remain_cube * remain * (4.0 * radius + 1.0), -10.0 * remain_cube)

def reference(x_points, z_points, length_scales, dpsi_grad, block_rows, block_cols, block_count):
    highest = lax.Precision.HIGHEST
    float_type = x_points.dtype
    total_slots = ROW_GROUPS * COL_GROUPS * CAP
    total_blocks = COL_GROUPS * CB_DEV
    live_all = jnp.arange(CAP, dtype=jnp.int32)[None, None, :] < block_count[:, :, None]
    z_blocks = z_points.reshape(Q, total_blocks, BS)
    group_ids = jnp.arange(COL_GROUPS, dtype=jnp.int32)

    def one_slot(flat_index):
        row_group = flat_index // (COL_GROUPS * CAP)
        column_group = flat_index // CAP % COL_GROUPS
        slot_index = flat_index % CAP
        row_local = block_rows[row_group, column_group, slot_index]
        col_local = block_cols[row_group, column_group, slot_index]
        live_weight = live_all[row_group, column_group, slot_index].astype(float_type)
        row_start = ((row_group * RB_DEV + row_local) * BS).astype(jnp.int32)
        col_start = ((column_group * CB_DEV + col_local) * BS).astype(jnp.int32)
        x_rows = lax.dynamic_slice_in_dim(x_points, row_start, BS, 1)
        z_cols = lax.dynamic_slice_in_dim(z_points, col_start, BS, 1)
        matched = live_all[row_group] & (block_rows[row_group] == row_local)
        near_weight = jnp.any(matched, axis=1).astype(float_type)
        near_local = lax.optimization_barrier(jnp.sum(jnp.where(matched, block_cols[row_group], 0), axis=1)).astype(jnp.int32)
        near_blocks = (group_ids * CB_DEV + near_local).astype(jnp.int32)
        z_near = z_blocks[:, near_blocks, :].reshape(Q, COL_GROUPS * BS)
        kernel, _ = wendland(x_rows, z_near, length_scales)
        masked = kernel * jnp.repeat(near_weight, BS)[None, :]
        near_starts = (near_blocks * BS).astype(jnp.int32)

        def pick_tile(row_at):
            return lax.dynamic_slice(dpsi_grad, (row_at, col_start), (BS, BS))
        near_tiles = jax.vmap(pick_tile)(near_starts).reshape(COL_GROUPS * BS, BS)
        dk_block = jnp.dot(masked, near_tiles, precision=highest) * live_weight
        _, slopes = wendland(x_rows, z_cols, length_scales)
        grad_k = dk_block * slopes
        col_sum = lax.optimization_barrier(jnp.sum(grad_k, axis=0))
        x_weighted = jnp.dot(x_rows, grad_k, precision=highest)
        z_part = (-2.0 / (length_scales * length_scales))[:, None] * (x_weighted - z_cols * col_sum[None, :])
        scale_terms = []
        for dim_q in range(x_rows.shape[0]):
            offset = x_rows[dim_q][:, None] - z_cols[dim_q][None, :]
            scale_terms.append(jnp.sum(grad_k * offset * offset))
        cube_scale = length_scales * length_scales * length_scales
        scale_part = -2.0 / cube_scale * jnp.stack(scale_terms)
        onehot = (jnp.arange(total_blocks, dtype=jnp.int32) == (column_group * CB_DEV + col_local).astype(jnp.int32)).astype(float_type)
        return (dk_block, z_part, scale_part, onehot)
    dk_all, z_parts, scale_parts, onehots = lax.map(one_slot, jnp.arange(total_slots, dtype=jnp.int32))
    z_grad = jnp.einsum('sm,sqb->qmb', onehots, z_parts, precision=highest).reshape(x_points.shape[0], M)
    scale_grad = lax.optimization_barrier(jnp.sum(scale_parts, axis=0))
    return (dk_all.reshape(ROW_GROUPS, COL_GROUPS, CAP, BS, BS), z_grad, scale_grad)
```

```python
import itertools

import jax
import jax.numpy as jnp
from jax import lax
from jax.experimental import pallas as pl
from jax.experimental.pallas import tpu as pltpu
from jax.sharding import Mesh, PartitionSpec as P

BS = 256
SLOTS = 3
AXES = ("xh", "y", "c", "xl", "z")
SIZES = (2, 4, 2, 2, 4)
DP = ("xh", "y", "c")
IND = ("xl", "z")


def pairs(target):
    def flat(place):
        index = 0
        for size, coord in zip(SIZES, place):
            index = index * size + coord
        return index

    places = itertools.product(*(range(size) for size in SIZES))
    return [(flat(place), flat(target(*place))) for place in places]


def shift_y(step):
    return pairs(lambda xh, y, c, xl, z: (xh, (y + step) % 4, c, xl, z))


SWAP_CORE = pairs(lambda xh, y, c, xl, z: (xh, y, 1 - c, xl, z))
SWAP_XH = pairs(lambda xh, y, c, xl, z: (1 - xh, y, c, xl, z))
Y_UP = shift_y(1)
Y_DOWN = shift_y(3)


def transpose_place(xh, y, c, xl, z):
    row = (xh * 4 + y) * 2 + c
    col = xl * 4 + z
    owner, new_col = 2 * col + row % 2, row // 2
    return (owner // 8, owner // 2 % 4, owner % 2, new_col // 4, new_col % 4)


TRANSPOSE = pairs(transpose_place)


def permute(value, perm):
    return lax.ppermute(value, AXES, perm)


def payload_kernel(rows_ref, cols_ref, count_ref, x_ref, out_ref, pack_ref):
    lane = lax.broadcasted_iota(jnp.int32, (1, BS), 1)
    pack_ref[...] = jnp.zeros_like(pack_ref)
    for slot in range(SLOTS):
        live = jnp.where(count_ref[0] > slot, 1, 0)
        row = rows_ref[slot] * live
        col = cols_ref[slot] * live
        start = pl.multiple_of(row * BS, BS)
        pack_ref[4 * slot : 4 * slot + 3, :] = x_ref[:, pl.ds(start, BS)]
        info = jnp.where(lane == 0, row, jnp.where(lane == 1, col, jnp.where(lane == 2, live, 0)))
        pack_ref[4 * slot + 3 : 4 * slot + 4, :] = info.astype(jnp.float32)
    packed = pack_ref[...]
    for dest in range(out_ref.shape[0]):
        out_ref[dest] = packed


def slot_of(place, step, own_ref, near_ref, pos_ref):
    own_x = place // SLOTS
    slot = place % SLOTS
    xh = jnp.where(own_x == 1, pos_ref[0], 1 - pos_ref[0])
    group = xh * 8 + lax.rem(pos_ref[1] + step, 4) * 2 + pos_ref[2]
    base = group * 9
    row = own_ref[base + 3 * slot]
    col = own_ref[base + 3 * slot + 1]
    live = own_ref[base + 3 * slot + 2]
    near = 0
    found = 0
    for other in range(SLOTS):
        match = jnp.where(near_ref[base + 3 * other] == row, near_ref[base + 3 * other + 2], 0)
        near = near + match * near_ref[base + 3 * other + 1]
        found = found + match
    return group, slot, col, near, (live * found) > 0


def column_of(pay_ref, group, slot):
    rolled = pltpu.roll(pay_ref[group], lax.rem(16 - 4 * slot, 16), 0)
    padded = jnp.concatenate([rolled[0:8], jnp.zeros((120, BS), jnp.float32)], axis=0)
    return jnp.transpose(padded)


def split(value):
    high = value.astype(jnp.bfloat16)
    return high, (value - high.astype(jnp.float32)).astype(jnp.bfloat16)


def product_kernel(steps, own_ref, near_ref, pos_ref, scale_ref, pay_ref, z_ref, mine_ref, mate_ref,
                   out_ref, tiles, results, in_sems, out_sems):
    count = 2 * SLOTS

    def copy_in(source, row, col, place):
        window = source.at[pl.ds(row * BS, BS), pl.ds(col * BS, BS)]
        return pltpu.make_async_copy(window, tiles.at[place], in_sems.at[place])

    for number, step in enumerate(steps):
        for local in range(count):
            place = number * count + local
            _, _, col, near, active = slot_of(local, step, own_ref, near_ref, pos_ref)
            mine = (near // 4) == pos_ref[2]
            row = lax.rem(near, 4)

            @pl.when(jnp.logical_and(active, mine))
            def _():
                copy_in(mine_ref, row, col, place).start()

            @pl.when(jnp.logical_and(active, jnp.logical_not(mine)))
            def _():
                copy_in(mate_ref, row, col, place).start()

    for number, step in enumerate(steps):

        def body(local, carry):
            place = number * count + local
            group, slot, col, near, active = slot_of(local, step, own_ref, near_ref, pos_ref)

            @pl.when(active)
            def _():
                x_cols = column_of(pay_ref, group, slot)
                z_rows = z_ref[:, pl.ds(pl.multiple_of(near * BS, BS), BS)]
                dist = jnp.zeros((BS, BS), jnp.float32)
                for q in range(3):
                    offset = (x_cols[:, q : q + 1] - z_rows[q : q + 1, :]) * (1.0 / scale_ref[q])
                    dist = dist + offset * offset
                radius = jnp.sqrt(dist)
                remain = jnp.maximum(1.0 - radius, 0.0)
                square = remain * remain
                kernel = square * square * (4.0 * radius + 1.0)
                copy_in(mine_ref, 0, 0, place).wait()
                k_high, k_low = split(kernel)
                d_high, d_low = split(tiles[place])
                total = jnp.dot(k_high, d_low, preferred_element_type=jnp.float32)
                total = total + jnp.dot(k_low, d_high, preferred_element_type=jnp.float32)
                results[place] = total + jnp.dot(k_high, d_high, preferred_element_type=jnp.float32)

            @pl.when(jnp.logical_not(active))
            def _():
                results[place] = jnp.zeros((BS, BS), jnp.float32)

            pltpu.make_async_copy(results.at[place], out_ref.at[place], out_sems.at[place]).start()
            return carry

        lax.fori_loop(0, count, body, 0)

    for place in range(count * len(steps)):
        pltpu.make_async_copy(results.at[place], out_ref.at[place], out_sems.at[place]).wait()


def products(steps, tables, scales, payload, z_near, mine, mate):
    number = 2 * SLOTS * len(steps)
    smem = pl.BlockSpec(memory_space=pltpu.SMEM)
    vmem = pl.BlockSpec(memory_space=pltpu.VMEM)
    hbm = pl.BlockSpec(memory_space=pl.ANY)

    def kernel(*refs):
        product_kernel(steps, *refs)

    return pl.pallas_call(
        kernel,
        out_shape=jax.ShapeDtypeStruct((number, BS, BS), jnp.float32),
        in_specs=[smem, smem, smem, smem, vmem, vmem, hbm, hbm],
        out_specs=hbm,
        scratch_shapes=[
            pltpu.VMEM((number, BS, BS), jnp.float32),
            pltpu.VMEM((number, BS, BS), jnp.float32),
            pltpu.SemaphoreType.DMA((number,)),
            pltpu.SemaphoreType.DMA((number,)),
        ],
        name="products",
    )(*tables, scales, payload, z_near, mine, mate)


def gradient_kernel(plan, own_ref, near_ref, pos_ref, scale_ref, pay_ref, z_ref, *refs):
    parts, out_ref = refs[:-1], refs[-1]
    out_ref[...] = jnp.zeros_like(out_ref)
    count = 2 * SLOTS
    for part, steps in zip(parts, plan):
        for number, step in enumerate(steps):

            def body(local, carry):
                group, slot, col, near, active = slot_of(local, step, own_ref, near_ref, pos_ref)

                @pl.when(active)
                def _():
                    x_cols = column_of(pay_ref, group, slot)
                    start = pl.multiple_of(col * BS, BS)
                    z_rows = z_ref[:, pl.ds(start, BS)]
                    dist = jnp.zeros((BS, BS), jnp.float32)
                    offsets = []
                    for q in range(3):
                        offset = (x_cols[:, q : q + 1] - z_rows[q : q + 1, :]) * (1.0 / scale_ref[q])
                        offsets.append(offset)
                        dist = dist + offset * offset
                    remain = jnp.maximum(1.0 - jnp.sqrt(dist), 0.0)
                    grad = part[number * count + local] * (remain * remain * remain)
                    z_sums, scale_sums = [], []
                    for q in range(3):
                        weighted = grad * offsets[q]
                        factor = 20.0 / scale_ref[q]
                        z_sums.append(factor * jnp.sum(weighted, axis=0, keepdims=True))
                        scale_sums.append(factor * jnp.sum(weighted * offsets[q], axis=0, keepdims=True))
                    for q in range(3):
                        out_ref[q : q + 1, pl.ds(start, BS)] += z_sums[q]
                        out_ref[3:4, q * BS : (q + 1) * BS] += scale_sums[q]

                return carry

            lax.fori_loop(0, count, body, 0)


def gradients(plan, tables, scales, payload, z_own, parts):
    smem = pl.BlockSpec(memory_space=pltpu.SMEM)
    vmem = pl.BlockSpec(memory_space=pltpu.VMEM)

    def kernel(*refs):
        gradient_kernel(plan, *refs)

    return pl.pallas_call(
        kernel,
        out_shape=jax.ShapeDtypeStruct((4, z_own.shape[1]), jnp.float32),
        in_specs=[smem, smem, smem, smem, vmem, vmem] + [vmem] * len(parts),
        out_specs=vmem,
        name="gradients",
    )(*tables, scales, payload, z_own, *parts)


def on_device(x_points, z_points, length_scales, dpsi_grad, block_rows, block_cols, block_count):
    smem = pl.BlockSpec(memory_space=pltpu.SMEM)
    vmem = pl.BlockSpec(memory_space=pltpu.VMEM)
    xh, y, core = (lax.axis_index(name).astype(jnp.int32) for name in DP)
    mate = permute(dpsi_grad, SWAP_CORE)
    z_near = permute(z_points, TRANSPOSE)
    outgoing = pl.pallas_call(
        payload_kernel,
        out_shape=jax.ShapeDtypeStruct((16, 16, BS), jnp.float32),
        in_specs=[smem, smem, smem, vmem],
        out_specs=vmem,
        scratch_shapes=[pltpu.VMEM((16, BS), jnp.float32)],
        name="payload",
    )(block_rows.reshape(-1), block_cols.reshape(-1), block_count.reshape(-1), x_points)
    payload = lax.all_to_all(outgoing, DP, 0, 0, tiled=True)
    own_table = jnp.stack([payload[:, 4 * s + 3, :3] for s in range(SLOTS)], axis=1).reshape(16, 9)
    own_table = own_table.astype(jnp.int32)
    near_table = permute(own_table, TRANSPOSE)
    tables = (own_table.reshape(-1), near_table.reshape(-1), jnp.stack([xh, y, core]))

    plan = ((2,), (1, 3), (0,))
    args = (tables, length_scales, payload, z_near, dpsi_grad, mate)
    far = products(plan[0], *args)
    sides = products(plan[1], *args)
    here = products(plan[2], *args)

    half = BS // 2
    s3 = SLOTS
    far_o, far_w = far[:s3], far[s3:]
    up_o, up_w, down_o, down_w = (sides[k * s3 : (k + 1) * s3] for k in range(4))
    got_up_o = permute(far_o[:, :half], Y_UP)
    got_down_o = permute(far_o[:, half:], Y_DOWN)
    got_up_w = permute(far_w[:, :half], Y_UP)
    got_down_w = permute(far_w[:, half:], Y_DOWN)
    up_o = up_o.at[:, :half].add(got_up_o)
    down_o = down_o.at[:, half:].add(got_down_o)
    up_w = up_w.at[:, :half].add(got_up_w)
    down_w = down_w.at[:, half:].add(got_down_w)
    sum_o = here[:s3] + permute(up_o, Y_UP) + permute(down_o, Y_DOWN)
    got_x = permute(sum_o, SWAP_XH)
    sum_w = here[s3:] + permute(up_w, Y_UP) + permute(down_w, Y_DOWN)
    live = jnp.arange(s3, dtype=jnp.int32) < block_count[0, 0]
    dk_local = jnp.where(live[:, None, None], sum_w + got_x, 0.0)

    local = gradients(plan, tables, length_scales, payload, z_points, (far, sides, here))
    width = local.shape[1] // 16
    scale_part = jnp.sum(local[3, : 3 * BS].reshape(3, BS), axis=1)
    chunks = local[:3].reshape(3, 16, width).transpose(1, 0, 2)
    scale_row = jnp.broadcast_to(jnp.pad(scale_part, (0, width - 3))[None, None, :], (16, 1, width))
    chunks = jnp.concatenate([chunks, scale_row], axis=1)
    summed = jnp.sum(lax.all_to_all(chunks, DP, 0, 0, tiled=True), axis=0)
    spread = lax.all_to_all(jnp.broadcast_to(summed[None], (16, 4, width)), DP, 0, 0, tiled=True)
    z_grad = spread[:, :3].transpose(1, 0, 2).reshape(3, 16 * width)
    by_col = lax.all_to_all(jnp.broadcast_to(summed[3:4], (8, width)), IND, 0, 0, tiled=True)
    scale_grad = jnp.sum(by_col[:, :3], axis=0)
    return dk_local.reshape(1, 1, s3, BS, BS), z_grad, scale_grad


def solution(mesh):
    fine = Mesh(mesh.devices.reshape(SIZES), AXES)
    return jax.shard_map(
        on_device,
        mesh=fine,
        in_specs=(
            P(None, DP),
            P(None, IND),
            P(),
            P(DP, IND),
            P(DP, IND, None),
            P(DP, IND, None),
            P(DP, IND),
        ),
        out_specs=(P(DP, IND, None, None, None), P(None, IND), P()),
        check_vma=False,
    )
```

```python
import itertools

import jax
import jax.numpy as jnp
from jax import lax
from jax.experimental import pallas as pl
from jax.experimental.pallas import tpu as pltpu
from jax.sharding import Mesh, PartitionSpec as P


BS = 256
SLOTS = 3
AXES = ("xh", "y", "c", "xl", "z")
SIZES = (2, 4, 2, 2, 4)
DP = ("xh", "y", "c")
IND = ("xl", "z")


def pairs(target):
    def flat(place):
        index = 0
        for size, coord in zip(SIZES, place):
            index = index * size + coord
        return index

    places = itertools.product(*(range(size) for size in SIZES))
    return [(flat(place), flat(target(*place))) for place in places]


def shift_y(step):
    return pairs(lambda xh, y, c, xl, z: (xh, (y + step) % 4, c, xl, z))


SWAP_CORE = pairs(lambda xh, y, c, xl, z: (xh, y, 1 - c, xl, z))
SWAP_XH = pairs(lambda xh, y, c, xl, z: (1 - xh, y, c, xl, z))
SWAP_XL = pairs(lambda xh, y, c, xl, z: (xh, y, c, 1 - xl, z))


def flip_y(bits):
    return pairs(lambda xh, y, c, xl, z: (xh, y ^ bits, c, xl, z))


def flip_z(bits):
    return pairs(lambda xh, y, c, xl, z: (xh, y, c, xl, z ^ bits))


Y_UP = shift_y(1)
Y_DOWN = shift_y(3)


def transpose_place(xh, y, c, xl, z):
    row = (xh * 4 + y) * 2 + c
    col = xl * 4 + z
    owner, new_col = 2 * col + row % 2, row // 2
    return (owner // 8, owner // 2 % 4, owner % 2, new_col // 4, new_col % 4)


TRANSPOSE = pairs(transpose_place)


def permute(value, perm):
    return lax.ppermute(value, AXES, perm)


def payload_kernel(rows_ref, cols_ref, count_ref, x_ref, out_ref, pack_ref):
    lane = lax.broadcasted_iota(jnp.int32, (1, BS), 1)
    info = jnp.zeros((1, BS), jnp.int32)
    pack_ref[...] = jnp.zeros_like(pack_ref)
    for slot in range(SLOTS):
        live = jnp.where(count_ref[0, 0] > slot, 1, 0)
        row = rows_ref[0, 0, slot] * live
        col = cols_ref[0, 0, slot] * live
        start = pl.multiple_of(row * BS, BS)
        pack_ref[4 * slot : 4 * slot + 3, :] = x_ref[:, pl.ds(start, BS)]
        for place, value in enumerate((row, col, live)):
            info = jnp.where(lane == 3 * slot + place, value, info)
    pack_ref[12:13, :] = info.astype(jnp.float32)
    packed = pack_ref[...]
    for dest in range(out_ref.shape[0]):
        out_ref[dest] = packed


def slot_of(place, step, own_ref, near_ref, pos_ref):
    own_x = place // SLOTS
    slot = place % SLOTS
    xh = jnp.where(own_x == 1, pos_ref[0], 1 - pos_ref[0])
    group = xh * 8 + lax.rem(pos_ref[1] + step, 4) * 2 + pos_ref[2]
    row = own_ref[group, 3 * slot]
    col = own_ref[group, 3 * slot + 1]
    live = own_ref[group, 3 * slot + 2]
    near = 0
    found = 0
    for other in range(SLOTS):
        match = jnp.where(near_ref[group, 3 * other] == row, near_ref[group, 3 * other + 2], 0)
        near = near + match * near_ref[group, 3 * other + 1]
        found = found + match
    return group, slot, col, near, (live * found) > 0


def scaled_points(pay_ref, group, slot, z_ref, start, scale_ref):
    rolled = pltpu.roll(pay_ref[group], lax.rem(16 - 4 * slot, 16), 0)
    padded = jnp.concatenate([rolled[0:8], jnp.zeros((120, BS), jnp.float32)], axis=0)
    x_cols = jnp.transpose(padded)
    z_rows = z_ref[:, pl.ds(pl.multiple_of(start, BS), BS)]
    inverses = [1.0 / scale_ref[q] for q in range(3)]
    return [x_cols[:, q : q + 1] * inverses[q] for q in range(3)], [z_rows[q : q + 1, :] * inverses[q] for q in range(3)]


def strip_offsets(points, row):
    x_cols, z_rows = points
    return [x_cols[q][row : row + STRIP] - z_rows[q] for q in range(3)]


def radius_of(offsets):
    dist = offsets[0] * offsets[0] + offsets[1] * offsets[1] + offsets[2] * offsets[2]
    return dist * lax.rsqrt(jnp.maximum(dist, 1e-30))


def split(value):
    high = value.astype(jnp.bfloat16)
    return high, (value - high.astype(jnp.float32)).astype(jnp.bfloat16)


STRIP = 32
HALF = BS // 2
COUNT = 2 * SLOTS


def product_kernel(steps, form, own_ref, near_ref, pos_ref, scale_ref, pay_ref, z_ref, mine_ref, mate_ref, *refs):
    *outs, tiles, results, left, right, in_sems, out_sems = refs

    def copy_in(source, row, col, place):
        window = source.at[pl.ds(row * BS, BS), pl.ds(col * BS, BS)]
        return pltpu.make_async_copy(window, tiles.at[place], in_sems.at[place])

    def copy_half(place, half, out, index):
        window = results.at[place, pl.ds(half * HALF, HALF)]
        return pltpu.make_async_copy(window, out.at[index], out_sems.at[place, half])

    def copy_out(number, local, place):
        if form == "whole":
            for half in range(2):
                window = outs[0].at[local, pl.ds(half * HALF, HALF)]
                source = results.at[place, pl.ds(half * HALF, HALF)]
                pltpu.make_async_copy(source, window, out_sems.at[place, half]).start()
        elif form == "halves":
            for half in range(2):
                copy_half(place, half, outs[half], local).start()
        else:
            for own_x in range(2):

                @pl.when(local // SLOTS == own_x)
                def _():
                    for half in range(2):
                        out = outs[4 * number + 2 * own_x + half]
                        copy_half(place, half, out, local % SLOTS).start()

    for number, step in enumerate(steps):
        for local in range(COUNT):
            place = number * COUNT + local
            _, _, col, near, active = slot_of(local, step, own_ref, near_ref, pos_ref)
            mine = (near // 4) == pos_ref[2]
            row = lax.rem(near, 4)

            @pl.when(jnp.logical_and(active, mine))
            def _():
                copy_in(mine_ref, row, col, place).start()

            @pl.when(jnp.logical_and(active, jnp.logical_not(mine)))
            def _():
                copy_in(mate_ref, row, col, place).start()

    for number, step in enumerate(steps):

        def body(local, carry):
            place = number * COUNT + local
            group, slot, _, near, active = slot_of(local, step, own_ref, near_ref, pos_ref)

            @pl.when(active)
            def _():
                points = scaled_points(pay_ref, group, slot, z_ref, near * BS, scale_ref)
                for row in range(0, BS, STRIP):
                    rows = slice(row, row + STRIP)
                    radius = radius_of(strip_offsets(points, row))
                    remain = jnp.maximum(1.0 - radius, 0.0)
                    square = remain * remain
                    high, low = split(square * square * (4.0 * radius + 1.0))
                    left[rows, 0:BS] = high
                    left[rows, BS : 2 * BS] = low
                    left[rows, 2 * BS : 3 * BS] = high
                copy_in(mine_ref, 0, 0, place).wait()
                for row in range(0, BS, STRIP):
                    high, low = split(tiles[place, pl.ds(row, STRIP), :])
                    right[row : row + STRIP, :] = low
                    right[BS + row : BS + row + STRIP, :] = high
                    right[2 * BS + row : 2 * BS + row + STRIP, :] = high
                results[place] = jnp.dot(left[...], right[...], preferred_element_type=jnp.float32)

            @pl.when(jnp.logical_not(active))
            def _():
                results[place] = jnp.zeros((BS, BS), jnp.float32)

            copy_out(number, local, place)
            return carry

        lax.fori_loop(0, COUNT, body, 0)

    for place in range(COUNT * len(steps)):
        for half in range(2):
            window = results.at[place, pl.ds(half * HALF, HALF)]
            other = results.at[place, pl.ds((1 - half) * HALF, HALF)]
            pltpu.make_async_copy(window, other, out_sems.at[place, half]).wait()


SMEM = pl.BlockSpec(memory_space=pltpu.SMEM)
VMEM = pl.BlockSpec(memory_space=pltpu.VMEM)
HBM = pl.BlockSpec(memory_space=pl.ANY)


def products(steps, form, tables, scales, payload, z_near, mine, mate):
    number = COUNT * len(steps)
    shapes = {
        "whole": [(COUNT, BS, BS)],
        "halves": [(COUNT, HALF, BS)] * 2,
        "split": [(SLOTS, HALF, BS)] * (4 * len(steps)),
    }[form]

    def kernel(*refs):
        product_kernel(steps, form, *refs)

    return pl.pallas_call(
        kernel,
        out_shape=[jax.ShapeDtypeStruct(shape, jnp.float32) for shape in shapes],
        in_specs=[SMEM, SMEM, SMEM, SMEM, VMEM, VMEM, HBM, HBM],
        out_specs=[HBM] * len(shapes),
        scratch_shapes=[
            pltpu.VMEM((number, BS, BS), jnp.float32),
            pltpu.VMEM((number, BS, BS), jnp.float32),
            pltpu.VMEM((BS, 3 * BS), jnp.bfloat16),
            pltpu.VMEM((3 * BS, BS), jnp.bfloat16),
            pltpu.SemaphoreType.DMA((number,)),
            pltpu.SemaphoreType.DMA((number, 2)),
        ],
    )(*tables, scales, payload, z_near, mine, mate)


def gradient_kernel(own_ref, near_ref, pos_ref, scale_ref, pay_ref, z_ref, *refs):
    parts, out_ref = refs[:-1], refs[-1]
    out_ref[...] = jnp.zeros_like(out_ref)
    far, sides, here = parts[:2], parts[2:10], parts[10:]

    def accumulate(local, step, pick):
        group, slot, col, _, active = slot_of(local, step, own_ref, near_ref, pos_ref)

        @pl.when(active)
        def _():
            start = pl.multiple_of(col * BS, BS)
            points = scaled_points(pay_ref, group, slot, z_ref, start, scale_ref)
            z_sums = [jnp.zeros((8, BS), jnp.float32) for _ in range(3)]
            scale_sums = list(z_sums)
            for row in range(0, BS, STRIP):
                offsets = strip_offsets(points, row)
                remain = jnp.maximum(1.0 - radius_of(offsets), 0.0)
                grad = pick(row) * (remain * remain * remain)
                for q in range(3):
                    weighted = grad * offsets[q]
                    squared = weighted * offsets[q]
                    for piece in range(0, STRIP, 8):
                        z_sums[q] = z_sums[q] + weighted[piece : piece + 8]
                        scale_sums[q] = scale_sums[q] + squared[piece : piece + 8]
            for q in range(3):
                factor = 20.0 / scale_ref[q]
                out_ref[q : q + 1, pl.ds(start, BS)] += factor * jnp.sum(z_sums[q], axis=0, keepdims=True)
                out_ref[3:4, q * BS : (q + 1) * BS] += factor * jnp.sum(scale_sums[q], axis=0, keepdims=True)

    def both(top, bottom, index):
        def pick(row):
            source = top if row < HALF else bottom
            return source[index, pl.ds(row % HALF, STRIP), :]

        return pick

    def body(local, carry):
        accumulate(local, 2, both(far[0], far[1], local))
        accumulate(local, 0, lambda row: here[0][local, pl.ds(row, STRIP), :])
        return carry

    lax.fori_loop(0, COUNT, body, 0)

    def side_body(slot, carry):
        for number, step in enumerate((1, 3)):
            for own_x in range(2):
                top, bottom = sides[4 * number + 2 * own_x : 4 * number + 2 * own_x + 2]
                accumulate(own_x * SLOTS + slot, step, both(top, bottom, slot))
        return carry

    lax.fori_loop(0, SLOTS, side_body, 0)


def gradients(tables, scales, payload, z_own, parts):
    return pl.pallas_call(
        gradient_kernel,
        out_shape=jax.ShapeDtypeStruct((4, z_own.shape[1]), jnp.float32),
        in_specs=[SMEM, SMEM, SMEM, SMEM, VMEM, VMEM] + [VMEM] * len(parts),
        out_specs=VMEM,
        name="gradients",
    )(*tables, scales, payload, z_own, *parts)


def combine_kernel(base_ref, tops, bottoms, extra, count_ref, out_ref):
    slot = pl.program_id(0)
    keep = count_ref[0, 0] > slot
    for half, pieces in enumerate((tops, bottoms)):
        rows = pl.ds(half * HALF, HALF)
        total = base_ref[0, rows, :]
        for piece in pieces:
            total = total + piece[0]
        if extra is not None:
            total = jnp.where(keep, total + extra[0, rows, :], 0.0)
        out_ref[0, rows, :] = total


def combine(base, first, tops, bottoms, extra, count):
    whole = pl.BlockSpec((1, BS, BS), lambda s: (s, 0, 0))
    half = pl.BlockSpec((1, HALF, BS), lambda s: (s, 0, 0))
    extras = [] if extra is None else [extra]

    def kernel(count_ref, base_ref, *refs):
        extra_ref = refs[4] if extras else None
        combine_kernel(base_ref, refs[0:2], refs[2:4], extra_ref, count_ref, refs[-1])

    return pl.pallas_call(
        kernel,
        grid=(SLOTS,),
        out_shape=jax.ShapeDtypeStruct((SLOTS, BS, BS), jnp.float32),
        in_specs=[SMEM, pl.BlockSpec((1, BS, BS), lambda s: (s + first, 0, 0))] + [half] * 4 + [whole] * len(extras),
        out_specs=whole,
    )(count, base, *tops, *bottoms, *extras)


def on_device(x_points, z_points, length_scales, dpsi_grad, block_rows, block_cols, block_count):
    xh, y, core = (lax.axis_index(name).astype(jnp.int32) for name in DP)
    mate = permute(dpsi_grad, SWAP_CORE)
    z_near = permute(z_points, TRANSPOSE)
    outgoing = pl.pallas_call(
        payload_kernel,
        out_shape=jax.ShapeDtypeStruct((16, 16, BS), jnp.float32),
        in_specs=[SMEM, SMEM, SMEM, VMEM],
        out_specs=VMEM,
        scratch_shapes=[pltpu.VMEM((16, BS), jnp.float32)],
        name="payload",
    )(block_rows, block_cols, block_count, x_points)
    payload = lax.all_to_all(outgoing, DP, 0, 0, tiled=True)
    own_table = payload[:, 12, :9].astype(jnp.int32)
    near_table = permute(own_table, TRANSPOSE)
    tables = (own_table, near_table, jnp.stack([xh, y, core]))

    args = (tables, length_scales, payload, z_near, dpsi_grad, mate)
    far = products((2,), "halves", *args)
    got_up = permute(far[0], Y_UP)
    got_down = permute(far[1], Y_DOWN)
    sides = products((1, 3), "split", *args)
    up_o, up_w, down_o, down_w = (sides[2 * k : 2 * k + 2] for k in range(4))
    direct_up_o = permute(up_o[1], Y_UP)
    direct_down_o = permute(down_o[0], Y_DOWN)
    (here,) = products((0,), "whole", *args)
    local = gradients(tables, length_scales, payload, z_points, (*far, *sides, here))
    sum_up_o = permute(up_o[0] + got_up[:SLOTS], Y_UP)
    sum_down_o = permute(down_o[1] + got_down[:SLOTS], Y_DOWN)
    direct_up_w = permute(up_w[1], Y_UP)
    direct_down_w = permute(down_w[0], Y_DOWN)
    sum_up_w = permute(up_w[0] + got_up[SLOTS:], Y_UP)
    sum_down_w = permute(down_w[1] + got_down[SLOTS:], Y_DOWN)
    sum_o = combine(here, 0, (sum_up_o, direct_down_o), (direct_up_o, sum_down_o), None, block_count)
    got_x = permute(sum_o, SWAP_XH)
    dk_local = combine(here, SLOTS, (sum_up_w, direct_down_w), (direct_up_w, sum_down_w), got_x, block_count)

    total = local + permute(local, SWAP_CORE)
    total = total + permute(total, SWAP_XH)
    total = (total + permute(total, flip_y(1))) + (permute(total, flip_y(2)) + permute(total, flip_y(3)))
    z_grad = total[:3]
    scale = jnp.pad(jnp.sum(total[3, : 3 * BS].reshape(3, BS), axis=1), (0, 125)).reshape(1, 128)
    scale = (scale + permute(scale, flip_z(1))) + (permute(scale, flip_z(2)) + permute(scale, flip_z(3)))
    scale = scale + permute(scale, SWAP_XL)
    scale_grad = scale[0, :3]
    return dk_local.reshape(1, 1, SLOTS, BS, BS), z_grad, scale_grad


def solution(mesh):
    fine = Mesh(mesh.devices.reshape(SIZES), AXES)

    return jax.shard_map(
        on_device,
        mesh=fine,
        in_specs=(
            P(None, DP),
            P(None, IND),
            P(),
            P(DP, IND),
            P(DP, IND, None),
            P(DP, IND, None),
            P(DP, IND),
        ),
        out_specs=(P(DP, IND, None, None, None), P(None, IND), P()),
        check_vma=False,
    )
```

```python
import itertools

import jax
import jax.numpy as jnp
from jax import lax
from jax.experimental import pallas as pl
from jax.experimental.pallas import tpu as pltpu
from jax.sharding import Mesh, PartitionSpec as P


BS = 256
SLOTS = 3
AXES = ("xh", "y", "c", "xl", "z")
SIZES = (2, 4, 2, 2, 4)
DP = ("xh", "y", "c")
IND = ("xl", "z")


def pairs(target):
    def flat(place):
        index = 0
        for size, coord in zip(SIZES, place):
            index = index * size + coord
        return index

    places = itertools.product(*(range(size) for size in SIZES))
    return [(flat(place), flat(target(*place))) for place in places]


def shift_y(step):
    return pairs(lambda xh, y, c, xl, z: (xh, (y + step) % 4, c, xl, z))


SWAP_CORE = pairs(lambda xh, y, c, xl, z: (xh, y, 1 - c, xl, z))
SWAP_XH = pairs(lambda xh, y, c, xl, z: (1 - xh, y, c, xl, z))
SWAP_XL = pairs(lambda xh, y, c, xl, z: (xh, y, c, 1 - xl, z))


def flip_y(bits):
    return pairs(lambda xh, y, c, xl, z: (xh, y ^ bits, c, xl, z))


def flip_z(bits):
    return pairs(lambda xh, y, c, xl, z: (xh, y, c, xl, z ^ bits))


Y_UP = shift_y(1)
Y_DOWN = shift_y(3)


def transpose_place(xh, y, c, xl, z):
    row = (xh * 4 + y) * 2 + c
    col = xl * 4 + z
    owner, new_col = 2 * col + row % 2, row // 2
    return (owner // 8, owner // 2 % 4, owner % 2, new_col // 4, new_col % 4)


TRANSPOSE = pairs(transpose_place)


def permute(value, perm):
    return lax.ppermute(value, AXES, perm)


def payload_kernel(rows_ref, cols_ref, count_ref, x_ref, out_ref, pack_ref):
    lane = lax.broadcasted_iota(jnp.int32, (1, BS), 1)
    info = jnp.zeros((1, BS), jnp.int32)
    pack_ref[...] = jnp.zeros_like(pack_ref)
    for slot in range(SLOTS):
        live = jnp.where(count_ref[0, 0] > slot, 1, 0)
        row = rows_ref[0, 0, slot] * live
        col = cols_ref[0, 0, slot] * live
        start = pl.multiple_of(row * BS, BS)
        pack_ref[4 * slot : 4 * slot + 3, :] = x_ref[:, pl.ds(start, BS)]
        for place, value in enumerate((row, col, live)):
            info = jnp.where(lane == 3 * slot + place, value, info)
    pack_ref[12:13, :] = info.astype(jnp.float32)
    packed = pack_ref[...]
    for dest in range(out_ref.shape[0]):
        out_ref[dest] = packed


def slot_of(place, step, own_ref, near_ref, pos_ref):
    own_x = place // SLOTS
    slot = place % SLOTS
    xh = jnp.where(own_x == 1, pos_ref[0], 1 - pos_ref[0])
    group = xh * 8 + lax.rem(pos_ref[1] + step, 4) * 2 + pos_ref[2]
    row = own_ref[group, 3 * slot]
    col = own_ref[group, 3 * slot + 1]
    live = own_ref[group, 3 * slot + 2]
    near = 0
    found = 0
    for other in range(SLOTS):
        match = jnp.where(near_ref[group, 3 * other] == row, near_ref[group, 3 * other + 2], 0)
        near = near + match * near_ref[group, 3 * other + 1]
        found = found + match
    return group, slot, col, near, (live * found) > 0


def column_kernel(pos_ref, scale_ref, pay_ref, out_ref):
    lane = lax.broadcasted_iota(jnp.int32, (1, 128), 1)
    inverse = jnp.zeros((1, 128), jnp.float32)
    for q in range(3):
        inverse = jnp.where(lane == q, 1.0 / scale_ref[q], inverse)
    for chip in range(8):
        padded = jnp.concatenate([pay_ref[2 * chip + pos_ref[2]], jnp.zeros((112, BS), jnp.float32)], axis=0)
        turned = jnp.transpose(padded)
        for slot in range(SLOTS):
            shifted = turned if slot == 0 else pltpu.roll(turned, 128 - 4 * slot, 1)
            out_ref[chip, slot] = shifted * inverse


def scaled_points(cols_ref, group, slot, z_ref, start, scale_ref):
    z_rows = z_ref[:, pl.ds(pl.multiple_of(start, BS), BS)]
    z_rows = [z_rows[q : q + 1, :] * (1.0 / scale_ref[q]) for q in range(3)]

    def x_strip(row):
        block = cols_ref[group // 2, slot, pl.ds(row, STRIP), :]
        return [block[:, q : q + 1] for q in range(3)]

    return x_strip, z_rows


def strip_offsets(points, row):
    x_strip, z_rows = points
    x_cols = x_strip(row)
    return [x_cols[q] - z_rows[q] for q in range(3)]


def radius_of(offsets):
    dist = offsets[0] * offsets[0] + offsets[1] * offsets[1] + offsets[2] * offsets[2]
    return dist * lax.rsqrt(jnp.maximum(dist, 1e-30))


def split(value):
    high = value.astype(jnp.bfloat16)
    return high, (value - high.astype(jnp.float32)).astype(jnp.bfloat16)


STRIP = 32
HALF = BS // 2
COUNT = 2 * SLOTS


def product_kernel(steps, form, own_ref, near_ref, pos_ref, scale_ref, pay_ref, z_ref, mine_ref, mate_ref, *refs):
    *outs, tiles, left, right, in_sems = refs

    def copy_in(source, row, col, place):
        window = source.at[pl.ds(row * BS, BS), pl.ds(col * BS, BS)]
        return pltpu.make_async_copy(window, tiles.at[place], in_sems.at[place])

    def store(number, own_x, slot, half, value):
        if form == "whole":
            outs[0][own_x * SLOTS + slot, pl.ds(half * HALF, HALF), :] = value
        elif form == "halves":
            outs[half][own_x * SLOTS + slot] = value
        else:
            outs[4 * number + 2 * own_x + half][slot] = value

    for number, step in enumerate(steps):
        for local in range(COUNT):
            place = number * COUNT + local
            _, _, col, near, active = slot_of(local, step, own_ref, near_ref, pos_ref)
            mine = (near // 4) == pos_ref[2]
            row = lax.rem(near, 4)

            @pl.when(jnp.logical_and(active, mine))
            def _():
                copy_in(mine_ref, row, col, place).start()

            @pl.when(jnp.logical_and(active, jnp.logical_not(mine)))
            def _():
                copy_in(mate_ref, row, col, place).start()

    def block(number, step, own_x):
        def body(slot, carry):
            local = own_x * SLOTS + slot
            place = number * COUNT + local
            group, _, _, near, active = slot_of(local, step, own_ref, near_ref, pos_ref)

            @pl.when(active)
            def _():
                points = scaled_points(pay_ref, group, slot, z_ref, near * BS, scale_ref)
                copy_in(mine_ref, 0, 0, place).wait()
                for row in range(0, BS, STRIP):
                    high, low = split(tiles[place, pl.ds(row, STRIP), :])
                    right[row : row + STRIP, :] = low
                    right[BS + row : BS + row + STRIP, :] = high
                    right[2 * BS + row : 2 * BS + row + STRIP, :] = high
                for half in range(2):
                    for row in range(half * HALF, (half + 1) * HALF, STRIP):
                        rows = slice(row, row + STRIP)
                        radius = radius_of(strip_offsets(points, row))
                        remain = jnp.maximum(1.0 - radius, 0.0)
                        square = remain * remain
                        high, low = split(square * square * (4.0 * radius + 1.0))
                        left[rows, 0:BS] = high
                        left[rows, BS : 2 * BS] = low
                        left[rows, 2 * BS : 3 * BS] = high
                    rows = pl.ds(half * HALF, HALF)
                    value = jnp.dot(left[rows, :], right[...], preferred_element_type=jnp.float32)
                    store(number, own_x, slot, half, value)

            @pl.when(jnp.logical_not(active))
            def _():
                for half in range(2):
                    store(number, own_x, slot, half, jnp.zeros((HALF, BS), jnp.float32))

            return carry

        lax.fori_loop(0, SLOTS, body, 0)

    for number, step in enumerate(steps):
        for own_x in range(2):
            block(number, step, own_x)


def grant(mebibytes):
    return pltpu.CompilerParams(vmem_limit_bytes=mebibytes << 20)


SMEM = pl.BlockSpec(memory_space=pltpu.SMEM)
VMEM = pl.BlockSpec(memory_space=pltpu.VMEM)
HBM = pl.BlockSpec(memory_space=pl.ANY)
FAR_MEMORY = pl.BlockSpec(memory_space=pltpu.HBM)


def products(steps, form, tables, scales, payload, z_near, mine, mate):
    number = COUNT * len(steps)
    shapes = {
        "whole": [(COUNT, BS, BS)],
        "halves": [(COUNT, HALF, BS)] * 2,
        "split": [(SLOTS, HALF, BS)] * (4 * len(steps)),
    }[form]

    def kernel(*refs):
        product_kernel(steps, form, *refs)

    return pl.pallas_call(
        kernel,
        out_shape=[pltpu.VMEM(shape, jnp.float32) for shape in shapes],
        in_specs=[SMEM, SMEM, SMEM, SMEM, VMEM, VMEM, FAR_MEMORY, FAR_MEMORY],
        out_specs=[VMEM] * len(shapes),
        scratch_shapes=[
            pltpu.VMEM((number, BS, BS), jnp.float32),
            pltpu.VMEM((BS, 3 * BS), jnp.bfloat16),
            pltpu.VMEM((3 * BS, BS), jnp.bfloat16),
            pltpu.SemaphoreType.DMA((number,)),
        ],
        compiler_params=grant(4 + number),
    )(*tables, scales, payload, z_near, mine, mate)


def gradient_kernel(own_ref, near_ref, pos_ref, scale_ref, pay_ref, z_ref, *refs):
    parts, out_ref = refs[:-1], refs[-1]
    out_ref[...] = jnp.zeros_like(out_ref)
    far, sides, here = parts[:2], parts[2:10], parts[10:]

    def accumulate(local, step, pick):
        group, slot, col, _, active = slot_of(local, step, own_ref, near_ref, pos_ref)

        @pl.when(active)
        def _():
            start = pl.multiple_of(col * BS, BS)
            points = scaled_points(pay_ref, group, slot, z_ref, start, scale_ref)
            z_sums = [jnp.zeros((8, BS), jnp.float32) for _ in range(3)]
            scale_sums = list(z_sums)
            for row in range(0, BS, STRIP):
                offsets = strip_offsets(points, row)
                remain = jnp.maximum(1.0 - radius_of(offsets), 0.0)
                grad = pick(row) * (remain * remain * remain)
                for q in range(3):
                    weighted = grad * offsets[q]
                    squared = weighted * offsets[q]
                    for piece in range(0, STRIP, 8):
                        z_sums[q] = z_sums[q] + weighted[piece : piece + 8]
                        scale_sums[q] = scale_sums[q] + squared[piece : piece + 8]
            for q in range(3):
                factor = 20.0 / scale_ref[q]
                out_ref[q : q + 1, pl.ds(start, BS)] += factor * jnp.sum(z_sums[q], axis=0, keepdims=True)
                out_ref[3:4, q * BS : (q + 1) * BS] += factor * jnp.sum(scale_sums[q], axis=0, keepdims=True)

    def both(top, bottom, index):
        def pick(row):
            source = top if row < HALF else bottom
            return source[index, pl.ds(row % HALF, STRIP), :]

        return pick

    def body(local, carry):
        accumulate(local, 2, both(far[0], far[1], local))
        accumulate(local, 0, lambda row: here[0][local, pl.ds(row, STRIP), :])
        return carry

    lax.fori_loop(0, COUNT, body, 0)

    def side_body(slot, carry):
        for number, step in enumerate((1, 3)):
            for own_x in range(2):
                top, bottom = sides[4 * number + 2 * own_x : 4 * number + 2 * own_x + 2]
                accumulate(own_x * SLOTS + slot, step, both(top, bottom, slot))
        return carry

    lax.fori_loop(0, SLOTS, side_body, 0)


def gradients(tables, scales, payload, z_own, parts):
    return pl.pallas_call(
        gradient_kernel,
        out_shape=jax.ShapeDtypeStruct((4, z_own.shape[1]), jnp.float32),
        in_specs=[SMEM, SMEM, SMEM, SMEM, VMEM, VMEM] + [VMEM] * len(parts),
        out_specs=VMEM,
        name="gradients",
        compiler_params=grant(16),
    )(*tables, scales, payload, z_own, *parts)


def combine_kernel(first, count_ref, base_ref, *refs):
    *pieces, out_ref, base, halves, total, in_sems, out_sems = refs
    extra = pieces[4] if len(pieces) == 5 else None

    def copies(slot):
        made = [pltpu.make_async_copy(base_ref.at[first + slot], base.at[0, slot], in_sems.at[slot, 0])]
        for number in range(4):
            made.append(pltpu.make_async_copy(pieces[number].at[slot], halves.at[number, slot], in_sems.at[slot, 1 + number]))
        if extra is not None:
            made.append(pltpu.make_async_copy(extra.at[slot], base.at[1, slot], in_sems.at[slot, 5]))
        return made

    for slot in range(SLOTS):
        for copy in copies(slot):
            copy.start()
    for slot in range(SLOTS):
        for copy in copies(slot):
            copy.wait()
        for half in range(2):
            rows = pl.ds(half * HALF, HALF)
            value = base[0, slot, rows, :] + halves[2 * half, slot] + halves[2 * half + 1, slot]
            if extra is not None:
                value = jnp.where(count_ref[0, 0] > slot, value + base[1, slot, rows, :], 0.0)
            total[slot, rows, :] = value
        pltpu.make_async_copy(total.at[slot], out_ref.at[slot], out_sems.at[slot]).start()
    for slot in range(SLOTS):
        pltpu.make_async_copy(total.at[slot], out_ref.at[slot], out_sems.at[slot]).wait()


def combine(base, first, tops, bottoms, extra, count):
    extras = [] if extra is None else [extra]

    def kernel(*refs):
        combine_kernel(first, *refs)

    return pl.pallas_call(
        kernel,
        out_shape=jax.ShapeDtypeStruct((SLOTS, BS, BS), jnp.float32),
        in_specs=[SMEM] + [HBM] * (5 + len(extras)),
        out_specs=HBM,
        scratch_shapes=[
            pltpu.VMEM((1 + len(extras), SLOTS, BS, BS), jnp.float32),
            pltpu.VMEM((4, SLOTS, HALF, BS), jnp.float32),
            pltpu.VMEM((SLOTS, BS, BS), jnp.float32),
            pltpu.SemaphoreType.DMA((SLOTS, 6)),
            pltpu.SemaphoreType.DMA((SLOTS,)),
        ],
        compiler_params=grant(8),
    )(count, base, *tops, *bottoms, *extras)


def on_device(x_points, z_points, length_scales, dpsi_grad, block_rows, block_cols, block_count):
    xh, y, core = (lax.axis_index(name).astype(jnp.int32) for name in DP)
    length_scales = pltpu.with_memory_space_constraint(length_scales, pltpu.HBM)
    mate = permute(dpsi_grad, SWAP_CORE)
    z_near = permute(z_points, TRANSPOSE)
    outgoing = pl.pallas_call(
        payload_kernel,
        out_shape=jax.ShapeDtypeStruct((16, 16, BS), jnp.float32),
        in_specs=[SMEM, SMEM, SMEM, VMEM],
        out_specs=VMEM,
        scratch_shapes=[pltpu.VMEM((16, BS), jnp.float32)],
        name="payload",
        compiler_params=grant(58),
    )(block_rows, block_cols, block_count, x_points)
    payload = lax.all_to_all(outgoing, DP, 0, 0, tiled=True)
    own_table = payload[:, 12, :9].astype(jnp.int32)
    near_table = permute(own_table, TRANSPOSE)
    tables = (own_table, near_table, jnp.stack([xh, y, core]))

    columns = pl.pallas_call(
        column_kernel,
        out_shape=pltpu.VMEM((8, SLOTS, BS, 128), jnp.float32),
        in_specs=[SMEM, SMEM, VMEM],
        out_specs=VMEM,
        name="columns",
        compiler_params=grant(8),
    )(tables[2], length_scales, payload)
    mine = pltpu.with_memory_space_constraint(dpsi_grad, pltpu.HBM)
    args = (tables, length_scales, columns, z_near, mine, mate)
    far = products((2,), "halves", *args)
    got_up = permute(far[0], Y_UP)
    got_down = permute(far[1], Y_DOWN)
    sides = products((1, 3), "split", *args)
    up_o, up_w, down_o, down_w = (sides[2 * k : 2 * k + 2] for k in range(4))
    direct_up_o = permute(up_o[1], Y_UP)
    direct_down_o = permute(down_o[0], Y_DOWN)
    (here,) = products((0,), "whole", *args)
    local = gradients(tables, length_scales, columns, z_points, (*far, *sides, here))
    sum_up_o = permute(up_o[0] + got_up[:SLOTS], Y_UP)
    sum_down_o = permute(down_o[1] + got_down[:SLOTS], Y_DOWN)
    direct_up_w = permute(up_w[1], Y_UP)
    direct_down_w = permute(down_w[0], Y_DOWN)
    sum_up_w = permute(up_w[0] + got_up[SLOTS:], Y_UP)
    sum_down_w = permute(down_w[1] + got_down[SLOTS:], Y_DOWN)
    sum_o = combine(here, 0, (sum_up_o, direct_down_o), (direct_up_o, sum_down_o), None, block_count)
    got_x = permute(sum_o, SWAP_XH)
    dk_local = combine(here, SLOTS, (sum_up_w, direct_down_w), (direct_up_w, sum_down_w), got_x, block_count)

    total = local + permute(local, SWAP_CORE)
    total = total + permute(total, SWAP_XH)
    total = (total + permute(total, flip_y(1))) + (permute(total, flip_y(2)) + permute(total, flip_y(3)))
    z_grad = total[:3]
    scale = jnp.pad(jnp.sum(total[3, : 3 * BS].reshape(3, BS), axis=1), (0, 125)).reshape(1, 128)
    scale = (scale + permute(scale, flip_z(1))) + (permute(scale, flip_z(2)) + permute(scale, flip_z(3)))
    scale = scale + permute(scale, SWAP_XL)
    scale_grad = scale[0, :3]
    return dk_local.reshape(1, 1, SLOTS, BS, BS), z_grad, scale_grad


def solution(mesh):
    fine = Mesh(mesh.devices.reshape(SIZES), AXES)

    return jax.shard_map(
        on_device,
        mesh=fine,
        in_specs=(
            P(None, DP),
            P(None, IND),
            P(),
            P(DP, IND),
            P(DP, IND, None),
            P(DP, IND, None),
            P(DP, IND),
        ),
        out_specs=(P(DP, IND, None, None, None), P(None, IND), P()),
        check_vma=False,
    )
```

```python
import itertools

import jax
import jax.numpy as jnp
from jax import lax
from jax.experimental import pallas as pl
from jax.experimental.pallas import tpu as pltpu
from jax.sharding import Mesh, PartitionSpec as P


BS = 256
SLOTS = 3
AXES = ("xh", "y", "c", "xl", "z")
SIZES = (2, 4, 2, 2, 4)
DP = ("xh", "y", "c")
IND = ("xl", "z")


def pairs(target):
    def flat(place):
        index = 0
        for size, coord in zip(SIZES, place):
            index = index * size + coord
        return index

    places = itertools.product(*(range(size) for size in SIZES))
    return [(flat(place), flat(target(*place))) for place in places]


def shift_y(step):
    return pairs(lambda xh, y, c, xl, z: (xh, (y + step) % 4, c, xl, z))


SWAP_CORE = pairs(lambda xh, y, c, xl, z: (xh, y, 1 - c, xl, z))
SWAP_XH = pairs(lambda xh, y, c, xl, z: (1 - xh, y, c, xl, z))
SWAP_XL = pairs(lambda xh, y, c, xl, z: (xh, y, c, 1 - xl, z))


def flip_y(bits):
    return pairs(lambda xh, y, c, xl, z: (xh, y ^ bits, c, xl, z))


def flip_z(bits):
    return pairs(lambda xh, y, c, xl, z: (xh, y, c, xl, z ^ bits))


Y_UP = shift_y(1)
Y_DOWN = shift_y(3)


def transpose_place(xh, y, c, xl, z):
    row = (xh * 4 + y) * 2 + c
    col = xl * 4 + z
    owner, new_col = 2 * col + row % 2, row // 2
    return (owner // 8, owner // 2 % 4, owner % 2, new_col // 4, new_col % 4)


TRANSPOSE = pairs(transpose_place)


def permute(value, perm):
    return lax.ppermute(value, AXES, perm)


def payload_kernel(rows_ref, cols_ref, count_ref, x_ref, out_ref, pack_ref):
    lane = lax.broadcasted_iota(jnp.int32, (1, BS), 1)
    info = jnp.zeros((1, BS), jnp.int32)
    pack_ref[...] = jnp.zeros_like(pack_ref)
    for slot in range(SLOTS):
        live = jnp.where(count_ref[0, 0] > slot, 1, 0)
        row = rows_ref[0, 0, slot] * live
        col = cols_ref[0, 0, slot] * live
        start = pl.multiple_of(row * BS, BS)
        pack_ref[4 * slot : 4 * slot + 3, :] = x_ref[:, pl.ds(start, BS)]
        for place, value in enumerate((row, col, live)):
            info = jnp.where(lane == 3 * slot + place, value, info)
    pack_ref[12:13, :] = info.astype(jnp.float32)
    packed = pack_ref[...]
    for dest in range(out_ref.shape[0]):
        out_ref[dest] = packed


def slot_of(place, step, own_ref, near_ref, pos_ref):
    own_x = place // SLOTS
    slot = place % SLOTS
    xh = jnp.where(own_x == 1, pos_ref[0], 1 - pos_ref[0])
    group = xh * 8 + lax.rem(pos_ref[1] + step, 4) * 2 + pos_ref[2]
    row = own_ref[group, 3 * slot]
    col = own_ref[group, 3 * slot + 1]
    live = own_ref[group, 3 * slot + 2]
    near = 0
    found = 0
    for other in range(SLOTS):
        match = jnp.where(near_ref[group, 3 * other] == row, near_ref[group, 3 * other + 2], 0)
        near = near + match * near_ref[group, 3 * other + 1]
        found = found + match
    return group, slot, col, near, (live * found) > 0


def column_kernel(pos_ref, scale_ref, pay_ref, out_ref):
    lane = lax.broadcasted_iota(jnp.int32, (1, 128), 1)
    inverse = jnp.zeros((1, 128), jnp.float32)
    for q in range(3):
        inverse = jnp.where(lane == q, 1.0 / scale_ref[q], inverse)
    for chip in range(8):
        padded = jnp.concatenate([pay_ref[2 * chip + pos_ref[2]], jnp.zeros((112, BS), jnp.float32)], axis=0)
        turned = jnp.transpose(padded)
        for slot in range(SLOTS):
            shifted = turned if slot == 0 else pltpu.roll(turned, 128 - 4 * slot, 1)
            out_ref[chip, slot] = shifted * inverse


def scaled_points(cols_ref, group, slot, z_ref, start, scale_ref):
    z_rows = z_ref[:, pl.ds(pl.multiple_of(start, BS), BS)]
    z_rows = [z_rows[q : q + 1, :] * (1.0 / scale_ref[q]) for q in range(3)]

    def x_strip(row):
        block = cols_ref[group // 2, slot, pl.ds(row, STRIP), :]
        return [block[:, q : q + 1] for q in range(3)]

    return x_strip, z_rows


def strip_offsets(points, row):
    x_strip, z_rows = points
    x_cols = x_strip(row)
    return [x_cols[q] - z_rows[q] for q in range(3)]


def radius_of(offsets):
    dist = offsets[0] * offsets[0] + offsets[1] * offsets[1] + offsets[2] * offsets[2]
    return dist * lax.rsqrt(jnp.maximum(dist, 1e-30))


def split(value):
    high = value.astype(jnp.bfloat16)
    return high, (value - high.astype(jnp.float32)).astype(jnp.bfloat16)


STRIP = 32
HALF = BS // 2
COUNT = 2 * SLOTS


def product_kernel(steps, form, own_ref, near_ref, pos_ref, scale_ref, pay_ref, z_ref, mine_ref, mate_ref, *refs):
    *outs, tiles, left, right, in_sems = refs

    def copy_in(source, row, col, place):
        window = source.at[pl.ds(row * BS, BS), pl.ds(col * BS, BS)]
        return pltpu.make_async_copy(window, tiles.at[place], in_sems.at[place])

    def store(number, own_x, slot, half, value):
        if form == "whole":
            outs[0][own_x * SLOTS + slot, pl.ds(half * HALF, HALF), :] = value
        elif form == "halves":
            outs[half][own_x * SLOTS + slot] = value
        else:
            outs[4 * number + 2 * own_x + half][slot] = value

    for number, step in enumerate(steps):
        for local in range(COUNT):
            place = number * COUNT + local
            _, _, col, near, active = slot_of(local, step, own_ref, near_ref, pos_ref)
            mine = (near // 4) == pos_ref[2]
            row = lax.rem(near, 4)

            @pl.when(jnp.logical_and(active, mine))
            def _():
                copy_in(mine_ref, row, col, place).start()

            @pl.when(jnp.logical_and(active, jnp.logical_not(mine)))
            def _():
                copy_in(mate_ref, row, col, place).start()

    def block(number, step, own_x):
        def body(slot, carry):
            local = own_x * SLOTS + slot
            place = number * COUNT + local
            group, _, _, near, active = slot_of(local, step, own_ref, near_ref, pos_ref)

            @pl.when(active)
            def _():
                points = scaled_points(pay_ref, group, slot, z_ref, near * BS, scale_ref)
                for half in range(2):
                    for row in range(half * HALF, (half + 1) * HALF, STRIP):
                        rows = slice(row, row + STRIP)
                        radius = radius_of(strip_offsets(points, row))
                        remain = jnp.maximum(1.0 - radius, 0.0)
                        square = remain * remain
                        high, low = split(square * square * (4.0 * radius + 1.0))
                        left[rows, 0:BS] = high
                        left[rows, BS : 2 * BS] = low
                        left[rows, 2 * BS : 3 * BS] = high
                copy_in(mine_ref, 0, 0, place).wait()
                for row in range(0, BS, STRIP):
                    high, low = split(tiles[place, pl.ds(row, STRIP), :])
                    right[row : row + STRIP, :] = low
                    right[BS + row : BS + row + STRIP, :] = high
                    right[2 * BS + row : 2 * BS + row + STRIP, :] = high
                for half in range(2):
                    rows = pl.ds(half * HALF, HALF)
                    value = jnp.dot(left[rows, :], right[...], preferred_element_type=jnp.float32)
                    store(number, own_x, slot, half, value)

            @pl.when(jnp.logical_not(active))
            def _():
                for half in range(2):
                    store(number, own_x, slot, half, jnp.zeros((HALF, BS), jnp.float32))

            return carry

        lax.fori_loop(0, SLOTS, body, 0)

    for number, step in enumerate(steps):
        for own_x in range(2):
            block(number, step, own_x)


def grant(mebibytes):
    return pltpu.CompilerParams(vmem_limit_bytes=mebibytes << 20)


SMEM = pl.BlockSpec(memory_space=pltpu.SMEM)
VMEM = pl.BlockSpec(memory_space=pltpu.VMEM)
HBM = pl.BlockSpec(memory_space=pl.ANY)
FAR_MEMORY = pl.BlockSpec(memory_space=pltpu.HBM)


def products(steps, form, tables, scales, payload, z_near, mine, mate):
    number = COUNT * len(steps)
    shapes = {
        "whole": [(COUNT, BS, BS)],
        "halves": [(COUNT, HALF, BS)] * 2,
        "split": [(SLOTS, HALF, BS)] * (4 * len(steps)),
    }[form]

    def kernel(*refs):
        product_kernel(steps, form, *refs)

    return pl.pallas_call(
        kernel,
        out_shape=[pltpu.VMEM(shape, jnp.float32) for shape in shapes],
        in_specs=[SMEM, SMEM, SMEM, SMEM, VMEM, VMEM, FAR_MEMORY, FAR_MEMORY],
        out_specs=[VMEM] * len(shapes),
        scratch_shapes=[
            pltpu.VMEM((number, BS, BS), jnp.float32),
            pltpu.VMEM((BS, 3 * BS), jnp.bfloat16),
            pltpu.VMEM((3 * BS, BS), jnp.bfloat16),
            pltpu.SemaphoreType.DMA((number,)),
        ],
        compiler_params=grant(4 + number),
    )(*tables, scales, payload, z_near, mine, mate)


def gradient_kernel(own_ref, near_ref, pos_ref, scale_ref, pay_ref, z_ref, *refs):
    parts, out_ref = refs[:-1], refs[-1]
    out_ref[...] = jnp.zeros_like(out_ref)
    far, sides, here = parts[:2], parts[2:10], parts[10:]

    def accumulate(local, step, pick):
        group, slot, col, _, active = slot_of(local, step, own_ref, near_ref, pos_ref)

        @pl.when(active)
        def _():
            start = pl.multiple_of(col * BS, BS)
            points = scaled_points(pay_ref, group, slot, z_ref, start, scale_ref)
            z_sums = [jnp.zeros((8, BS), jnp.float32) for _ in range(3)]
            scale_sums = list(z_sums)
            for row in range(0, BS, STRIP):
                offsets = strip_offsets(points, row)
                remain = jnp.maximum(1.0 - radius_of(offsets), 0.0)
                grad = pick(row) * (remain * remain * remain)
                for q in range(3):
                    weighted = grad * offsets[q]
                    squared = weighted * offsets[q]
                    for piece in range(0, STRIP, 8):
                        z_sums[q] = z_sums[q] + weighted[piece : piece + 8]
                        scale_sums[q] = scale_sums[q] + squared[piece : piece + 8]
            for q in range(3):
                factor = 20.0 / scale_ref[q]
                out_ref[q : q + 1, pl.ds(start, BS)] += factor * jnp.sum(z_sums[q], axis=0, keepdims=True)
                out_ref[3:4, q * BS : (q + 1) * BS] += factor * jnp.sum(scale_sums[q], axis=0, keepdims=True)

    def both(top, bottom, index):
        def pick(row):
            source = top if row < HALF else bottom
            return source[index, pl.ds(row % HALF, STRIP), :]

        return pick

    def body(local, carry):
        accumulate(local, 2, both(far[0], far[1], local))
        accumulate(local, 0, lambda row: here[0][local, pl.ds(row, STRIP), :])
        return carry

    lax.fori_loop(0, COUNT, body, 0)

    def side_body(slot, carry):
        for number, step in enumerate((1, 3)):
            for own_x in range(2):
                top, bottom = sides[4 * number + 2 * own_x : 4 * number + 2 * own_x + 2]
                accumulate(own_x * SLOTS + slot, step, both(top, bottom, slot))
        return carry

    lax.fori_loop(0, SLOTS, side_body, 0)


def gradients(tables, scales, payload, z_own, parts):
    return pl.pallas_call(
        gradient_kernel,
        out_shape=jax.ShapeDtypeStruct((4, z_own.shape[1]), jnp.float32),
        in_specs=[SMEM, SMEM, SMEM, SMEM, VMEM, VMEM] + [VMEM] * len(parts),
        out_specs=VMEM,
        name="gradients",
        compiler_params=grant(16),
    )(*tables, scales, payload, z_own, *parts)


def combine_kernel(first, base_ref, *refs):
    *pieces, out_ref, halves, in_sems = refs

    def copy(slot, number):
        return pltpu.make_async_copy(pieces[number].at[slot], halves.at[number, slot], in_sems.at[slot, number])

    for slot in range(SLOTS):
        for number in range(4):
            copy(slot, number).start()
    for slot in range(SLOTS):
        for number in range(4):
            copy(slot, number).wait()
        for half in range(2):
            rows = pl.ds(half * HALF, HALF)
            out_ref[slot, rows, :] = base_ref[first + slot, rows, :] + halves[2 * half, slot] + halves[2 * half + 1, slot]


def combine(base, first, tops, bottoms):
    def kernel(*refs):
        combine_kernel(first, *refs)

    return pl.pallas_call(
        kernel,
        out_shape=pltpu.VMEM((SLOTS, BS, BS), jnp.float32),
        in_specs=[VMEM] + [HBM] * 4,
        out_specs=VMEM,
        scratch_shapes=[
            pltpu.VMEM((4, SLOTS, HALF, BS), jnp.float32),
            pltpu.SemaphoreType.DMA((SLOTS, 4)),
        ],
        compiler_params=grant(8),
    )(base, *tops, *bottoms)


def on_device(x_points, z_points, length_scales, dpsi_grad, block_rows, block_cols, block_count):
    xh, y, core = (lax.axis_index(name).astype(jnp.int32) for name in DP)
    length_scales = pltpu.with_memory_space_constraint(length_scales, pltpu.HBM)
    mate = permute(dpsi_grad, SWAP_CORE)
    z_near = permute(z_points, TRANSPOSE)
    outgoing = pl.pallas_call(
        payload_kernel,
        out_shape=jax.ShapeDtypeStruct((16, 16, BS), jnp.float32),
        in_specs=[SMEM, SMEM, SMEM, VMEM],
        out_specs=VMEM,
        scratch_shapes=[pltpu.VMEM((16, BS), jnp.float32)],
        name="payload",
        compiler_params=grant(58),
    )(block_rows, block_cols, block_count, x_points)
    payload = lax.all_to_all(outgoing, DP, 0, 0, tiled=True)
    own_table = payload[:, 12, :9].astype(jnp.int32)
    near_table = permute(own_table, TRANSPOSE)
    tables = (own_table, near_table, jnp.stack([xh, y, core]))

    columns = pl.pallas_call(
        column_kernel,
        out_shape=pltpu.VMEM((8, SLOTS, BS, 128), jnp.float32),
        in_specs=[SMEM, SMEM, VMEM],
        out_specs=VMEM,
        name="columns",
        compiler_params=grant(8),
    )(tables[2], length_scales, payload)
    mine = pltpu.with_memory_space_constraint(dpsi_grad, pltpu.HBM)
    args = (tables, length_scales, columns, z_near, mine, mate)
    far = products((2,), "halves", *args)
    got_up = permute(far[0], Y_UP)
    got_down = permute(far[1], Y_DOWN)
    sides = products((1, 3), "split", *args)
    up_o, up_w, down_o, down_w = (sides[2 * k : 2 * k + 2] for k in range(4))
    direct_up_o = permute(up_o[1], Y_UP)
    direct_down_o = permute(down_o[0], Y_DOWN)
    (here,) = products((0,), "whole", *args)
    local = gradients(tables, length_scales, columns, z_points, (*far, *sides, here))
    sum_up_o = permute(up_o[0] + got_up[:SLOTS], Y_UP)
    sum_down_o = permute(down_o[1] + got_down[:SLOTS], Y_DOWN)
    direct_up_w = permute(up_w[1], Y_UP)
    direct_down_w = permute(down_w[0], Y_DOWN)
    sum_up_w = permute(up_w[0] + got_up[SLOTS:], Y_UP)
    sum_down_w = permute(down_w[1] + got_down[SLOTS:], Y_DOWN)
    sum_o = combine(here, 0, (sum_up_o, direct_down_o), (direct_up_o, sum_down_o))
    got_x = permute(sum_o, SWAP_XH)
    sum_w = combine(here, SLOTS, (sum_up_w, direct_down_w), (direct_up_w, sum_down_w))
    live = jnp.arange(SLOTS, dtype=jnp.int32)[:, None, None] < block_count
    dk_local = jnp.where(live, sum_w + got_x, 0.0)

    total = local + permute(local, SWAP_CORE)
    total = total + permute(total, SWAP_XH)
    total = (total + permute(total, flip_y(1))) + (permute(total, flip_y(2)) + permute(total, flip_y(3)))
    z_grad = total[:3]
    scale = jnp.pad(jnp.sum(total[3, : 3 * BS].reshape(3, BS), axis=1), (0, 125)).reshape(1, 128)
    scale = (scale + permute(scale, flip_z(1))) + (permute(scale, flip_z(2)) + permute(scale, flip_z(3)))
    scale = scale + permute(scale, SWAP_XL)
    scale_grad = scale[0, :3]
    return dk_local.reshape(1, 1, SLOTS, BS, BS), z_grad, scale_grad


def solution(mesh):
    fine = Mesh(mesh.devices.reshape(SIZES), AXES)

    return jax.shard_map(
        on_device,
        mesh=fine,
        in_specs=(
            P(None, DP),
            P(None, IND),
            P(),
            P(DP, IND),
            P(DP, IND, None),
            P(DP, IND, None),
            P(DP, IND),
        ),
        out_specs=(P(DP, IND, None, None, None), P(None, IND), P()),
        check_vma=False,
    )
```

```python
import itertools

import jax
import jax.numpy as jnp
from jax import lax
from jax.experimental import pallas as pl
from jax.experimental.pallas import tpu as pltpu
from jax.sharding import Mesh, PartitionSpec as P


BS = 256
SLOTS = 3
AXES = ("xh", "y", "c", "xl", "z")
SIZES = (2, 4, 2, 2, 4)
DP = ("xh", "y", "c")
IND = ("xl", "z")


def pairs(target):
    def flat(place):
        index = 0
        for size, coord in zip(SIZES, place):
            index = index * size + coord
        return index

    places = itertools.product(*(range(size) for size in SIZES))
    return [(flat(place), flat(target(*place))) for place in places]


def shift_y(step):
    return pairs(lambda xh, y, c, xl, z: (xh, (y + step) % 4, c, xl, z))


SWAP_CORE = pairs(lambda xh, y, c, xl, z: (xh, y, 1 - c, xl, z))
SWAP_XH = pairs(lambda xh, y, c, xl, z: (1 - xh, y, c, xl, z))
SWAP_XL = pairs(lambda xh, y, c, xl, z: (xh, y, c, 1 - xl, z))


def flip_y(bits):
    return pairs(lambda xh, y, c, xl, z: (xh, y ^ bits, c, xl, z))


def flip_z(bits):
    return pairs(lambda xh, y, c, xl, z: (xh, y, c, xl, z ^ bits))


Y_UP = shift_y(1)
Y_DOWN = shift_y(3)


def transpose_place(xh, y, c, xl, z):
    row = (xh * 4 + y) * 2 + c
    col = xl * 4 + z
    owner, new_col = 2 * col + row % 2, row // 2
    return (owner // 8, owner // 2 % 4, owner % 2, new_col // 4, new_col % 4)


TRANSPOSE = pairs(transpose_place)


def permute(value, perm):
    return lax.ppermute(value, AXES, perm)


def payload_kernel(rows_ref, cols_ref, count_ref, x_ref, out_ref, pack_ref):
    lane = lax.broadcasted_iota(jnp.int32, (1, BS), 1)
    info = jnp.zeros((1, BS), jnp.int32)
    pack_ref[...] = jnp.zeros_like(pack_ref)
    for slot in range(SLOTS):
        live = jnp.where(count_ref[0, 0] > slot, 1, 0)
        row = rows_ref[0, 0, slot] * live
        col = cols_ref[0, 0, slot] * live
        start = pl.multiple_of(row * BS, BS)
        pack_ref[4 * slot : 4 * slot + 3, :] = x_ref[:, pl.ds(start, BS)]
        for place, value in enumerate((row, col, live)):
            info = jnp.where(lane == 3 * slot + place, value, info)
    pack_ref[12:13, :] = info.astype(jnp.float32)
    packed = pack_ref[...]
    for dest in range(out_ref.shape[0]):
        out_ref[dest] = packed


def slot_of(place, step, own_ref, near_ref, pos_ref):
    own_x = place // SLOTS
    slot = place % SLOTS
    xh = jnp.where(own_x == 1, pos_ref[0], 1 - pos_ref[0])
    group = xh * 8 + lax.rem(pos_ref[1] + step, 4) * 2 + pos_ref[2]
    row = own_ref[group, 3 * slot]
    col = own_ref[group, 3 * slot + 1]
    live = own_ref[group, 3 * slot + 2]
    near = 0
    found = 0
    for other in range(SLOTS):
        match = jnp.where(near_ref[group, 3 * other] == row, near_ref[group, 3 * other + 2], 0)
        near = near + match * near_ref[group, 3 * other + 1]
        found = found + match
    return group, slot, col, near, (live * found) > 0


def column_kernel(pos_ref, scale_ref, pay_ref, out_ref):
    lane = lax.broadcasted_iota(jnp.int32, (1, 128), 1)
    inverse = jnp.zeros((1, 128), jnp.float32)
    for q in range(3):
        inverse = jnp.where(lane == q, 1.0 / scale_ref[q], inverse)
    for chip in range(8):
        padded = jnp.concatenate([pay_ref[2 * chip + pos_ref[2]], jnp.zeros((112, BS), jnp.float32)], axis=0)
        turned = jnp.transpose(padded)
        for slot in range(SLOTS):
            shifted = turned if slot == 0 else pltpu.roll(turned, 128 - 4 * slot, 1)
            out_ref[chip, slot] = shifted * inverse


def scaled_points(cols_ref, group, slot, z_ref, start, scale_ref):
    z_rows = z_ref[:, pl.ds(pl.multiple_of(start, BS), BS)]
    z_rows = [z_rows[q : q + 1, :] * (1.0 / scale_ref[q]) for q in range(3)]

    def x_strip(row):
        block = cols_ref[group // 2, slot, pl.ds(row, STRIP), :]
        return [block[:, q : q + 1] for q in range(3)]

    return x_strip, z_rows


def strip_offsets(points, row):
    x_strip, z_rows = points
    x_cols = x_strip(row)
    return [x_cols[q] - z_rows[q] for q in range(3)]


def radius_of(offsets):
    dist = offsets[0] * offsets[0] + offsets[1] * offsets[1] + offsets[2] * offsets[2]
    return dist * lax.rsqrt(jnp.maximum(dist, 1e-30))


def split(value):
    high = value.astype(jnp.bfloat16)
    return high, (value - high.astype(jnp.float32)).astype(jnp.bfloat16)


STRIP = 32
HALF = BS // 2
COUNT = 2 * SLOTS


def product_kernel(steps, form, own_ref, near_ref, pos_ref, scale_ref, pay_ref, z_ref, mine_ref, mate_ref, *refs):
    *outs, tiles, left, right, in_sems = refs

    def copy_in(source, row, col, place):
        window = source.at[pl.ds(row * BS, BS), pl.ds(col * BS, BS)]
        return pltpu.make_async_copy(window, tiles.at[place], in_sems.at[place])

    def store(number, own_x, slot, half, value):
        if form == "whole":
            outs[0][own_x * SLOTS + slot, pl.ds(half * HALF, HALF), :] = value
        elif form == "halves":
            outs[half][own_x * SLOTS + slot] = value
        else:
            outs[4 * number + 2 * own_x + half][slot] = value

    for number, step in enumerate(steps):
        for local in range(COUNT):
            place = number * COUNT + local
            _, _, col, near, active = slot_of(local, step, own_ref, near_ref, pos_ref)
            mine = (near // 4) == pos_ref[2]
            row = lax.rem(near, 4)

            @pl.when(jnp.logical_and(active, mine))
            def _():
                copy_in(mine_ref, row, col, place).start()

            @pl.when(jnp.logical_and(active, jnp.logical_not(mine)))
            def _():
                copy_in(mate_ref, row, col, place).start()

    def block(number, step, own_x):
        def body(slot, carry):
            local = own_x * SLOTS + slot
            place = number * COUNT + local
            group, _, _, near, active = slot_of(local, step, own_ref, near_ref, pos_ref)

            @pl.when(active)
            def _():
                points = scaled_points(pay_ref, group, slot, z_ref, near * BS, scale_ref)
                for half in range(2):
                    for row in range(half * HALF, (half + 1) * HALF, STRIP):
                        rows = slice(row, row + STRIP)
                        radius = radius_of(strip_offsets(points, row))
                        remain = jnp.maximum(1.0 - radius, 0.0)
                        square = remain * remain
                        high, low = split(square * square * (4.0 * radius + 1.0))
                        left[rows, 0:BS] = high
                        left[rows, BS : 2 * BS] = low
                        left[rows, 2 * BS : 3 * BS] = high
                copy_in(mine_ref, 0, 0, place).wait()
                for row in range(0, BS, STRIP):
                    high, low = split(tiles[place, pl.ds(row, STRIP), :])
                    right[row : row + STRIP, :] = low
                    right[BS + row : BS + row + STRIP, :] = high
                    right[2 * BS + row : 2 * BS + row + STRIP, :] = high
                for half in range(2):
                    rows = pl.ds(half * HALF, HALF)
                    value = jnp.dot(left[rows, :], right[...], preferred_element_type=jnp.float32)
                    store(number, own_x, slot, half, value)

            @pl.when(jnp.logical_not(active))
            def _():
                for half in range(2):
                    store(number, own_x, slot, half, jnp.zeros((HALF, BS), jnp.float32))

            return carry

        lax.fori_loop(0, SLOTS, body, 0)

    for number, step in enumerate(steps):
        for own_x in range(2):
            block(number, step, own_x)


def grant(mebibytes):
    return pltpu.CompilerParams(vmem_limit_bytes=mebibytes << 20)


SMEM = pl.BlockSpec(memory_space=pltpu.SMEM)
VMEM = pl.BlockSpec(memory_space=pltpu.VMEM)
HBM = pl.BlockSpec(memory_space=pl.ANY)
FAR_MEMORY = pl.BlockSpec(memory_space=pltpu.HBM)


def products(steps, form, tables, scales, payload, z_near, mine, mate):
    number = COUNT * len(steps)
    shapes = {
        "whole": [(COUNT, BS, BS)],
        "halves": [(COUNT, HALF, BS)] * 2,
        "split": [(SLOTS, HALF, BS)] * (4 * len(steps)),
    }[form]

    def kernel(*refs):
        product_kernel(steps, form, *refs)

    return pl.pallas_call(
        kernel,
        out_shape=[pltpu.VMEM(shape, jnp.float32) for shape in shapes],
        in_specs=[SMEM, SMEM, SMEM, SMEM, VMEM, VMEM, FAR_MEMORY, FAR_MEMORY],
        out_specs=[VMEM] * len(shapes),
        scratch_shapes=[
            pltpu.VMEM((number, BS, BS), jnp.float32),
            pltpu.VMEM((BS, 3 * BS), jnp.bfloat16),
            pltpu.VMEM((3 * BS, BS), jnp.bfloat16),
            pltpu.SemaphoreType.DMA((number,)),
        ],
        compiler_params=grant(4 + number),
    )(*tables, scales, payload, z_near, mine, mate)


def gradient_kernel(own_ref, near_ref, pos_ref, scale_ref, pay_ref, z_ref, *refs):
    parts, out_ref = refs[:-1], refs[-1]
    out_ref[...] = jnp.zeros_like(out_ref)
    far, sides, here = parts[:2], parts[2:10], parts[10:]

    def accumulate(local, step, pick):
        group, slot, col, _, active = slot_of(local, step, own_ref, near_ref, pos_ref)

        @pl.when(active)
        def _():
            start = pl.multiple_of(col * BS, BS)
            points = scaled_points(pay_ref, group, slot, z_ref, start, scale_ref)
            z_sums = [jnp.zeros((8, BS), jnp.float32) for _ in range(3)]
            scale_sums = list(z_sums)
            for row in range(0, BS, STRIP):
                offsets = strip_offsets(points, row)
                remain = jnp.maximum(1.0 - radius_of(offsets), 0.0)
                grad = pick(row) * (remain * remain * remain)
                for q in range(3):
                    weighted = grad * offsets[q]
                    squared = weighted * offsets[q]
                    for piece in range(0, STRIP, 8):
                        z_sums[q] = z_sums[q] + weighted[piece : piece + 8]
                        scale_sums[q] = scale_sums[q] + squared[piece : piece + 8]
            for q in range(3):
                factor = 20.0 / scale_ref[q]
                out_ref[q : q + 1, pl.ds(start, BS)] += factor * jnp.sum(z_sums[q], axis=0, keepdims=True)
                out_ref[3:4, q * BS : (q + 1) * BS] += factor * jnp.sum(scale_sums[q], axis=0, keepdims=True)

    def both(top, bottom, index):
        def pick(row):
            source = top if row < HALF else bottom
            return source[index, pl.ds(row % HALF, STRIP), :]

        return pick

    def body(local, carry):
        accumulate(local, 2, both(far[0], far[1], local))
        accumulate(local, 0, lambda row: here[0][local, pl.ds(row, STRIP), :])
        return carry

    lax.fori_loop(0, COUNT, body, 0)

    def side_body(slot, carry):
        for number, step in enumerate((1, 3)):
            for own_x in range(2):
                top, bottom = sides[4 * number + 2 * own_x : 4 * number + 2 * own_x + 2]
                accumulate(own_x * SLOTS + slot, step, both(top, bottom, slot))
        return carry

    lax.fori_loop(0, SLOTS, side_body, 0)


def gradients(tables, scales, payload, z_own, parts):
    return pl.pallas_call(
        gradient_kernel,
        out_shape=jax.ShapeDtypeStruct((4, z_own.shape[1]), jnp.float32),
        in_specs=[SMEM, SMEM, SMEM, SMEM, VMEM, VMEM] + [VMEM] * len(parts),
        out_specs=VMEM,
        name="gradients",
        compiler_params=grant(16),
    )(*tables, scales, payload, z_own, *parts)


def combine_kernel(first, base_ref, *refs):
    *pieces, out_ref, halves, in_sems = refs

    def copy(slot, number):
        return pltpu.make_async_copy(pieces[number].at[slot], halves.at[number, slot], in_sems.at[slot, number])

    for slot in range(SLOTS):
        for number in range(4):
            copy(slot, number).start()
    for slot in range(SLOTS):
        for number in range(4):
            copy(slot, number).wait()
        for half in range(2):
            rows = pl.ds(half * HALF, HALF)
            out_ref[slot, rows, :] = base_ref[first + slot, rows, :] + halves[2 * half, slot] + halves[2 * half + 1, slot]


def combine(base, first, tops, bottoms):
    def kernel(*refs):
        combine_kernel(first, *refs)

    return pl.pallas_call(
        kernel,
        out_shape=pltpu.VMEM((SLOTS, BS, BS), jnp.float32),
        in_specs=[VMEM] + [HBM] * 4,
        out_specs=VMEM,
        scratch_shapes=[
            pltpu.VMEM((4, SLOTS, HALF, BS), jnp.float32),
            pltpu.SemaphoreType.DMA((SLOTS, 4)),
        ],
        compiler_params=grant(8),
    )(base, *tops, *bottoms)


def finish_kernel(count_ref, base_ref, extra_ref, out_ref, extra, total, in_sems, out_sems):
    def fetch(slot):
        return pltpu.make_async_copy(extra_ref.at[slot], extra.at[slot], in_sems.at[slot])

    def put(slot):
        return pltpu.make_async_copy(total.at[slot], out_ref.at[slot], out_sems.at[slot])

    for slot in range(SLOTS):
        fetch(slot).start()
    for slot in range(SLOTS):
        fetch(slot).wait()
        total[slot] = jnp.where(count_ref[0, 0] > slot, base_ref[slot] + extra[slot], 0.0)
        put(slot).start()
    for slot in range(SLOTS):
        put(slot).wait()


def finish(base, extra, count):
    block = pltpu.VMEM((SLOTS, BS, BS), jnp.float32)
    return pl.pallas_call(
        finish_kernel,
        out_shape=jax.ShapeDtypeStruct((SLOTS, BS, BS), jnp.float32),
        in_specs=[SMEM, VMEM, HBM],
        out_specs=HBM,
        scratch_shapes=[block, block, pltpu.SemaphoreType.DMA((SLOTS,)), pltpu.SemaphoreType.DMA((SLOTS,))],
        name="finish",
        compiler_params=grant(8),
    )(count, base, extra)


def on_device(x_points, z_points, length_scales, dpsi_grad, block_rows, block_cols, block_count):
    xh, y, core = (lax.axis_index(name).astype(jnp.int32) for name in DP)
    length_scales = pltpu.with_memory_space_constraint(length_scales, pltpu.HBM)
    mate = permute(dpsi_grad, SWAP_CORE)
    z_near = permute(z_points, TRANSPOSE)
    outgoing = pl.pallas_call(
        payload_kernel,
        out_shape=jax.ShapeDtypeStruct((16, 16, BS), jnp.float32),
        in_specs=[SMEM, SMEM, SMEM, VMEM],
        out_specs=VMEM,
        scratch_shapes=[pltpu.VMEM((16, BS), jnp.float32)],
        name="payload",
        compiler_params=grant(58),
    )(block_rows, block_cols, block_count, x_points)
    payload = lax.all_to_all(outgoing, DP, 0, 0, tiled=True)
    own_table = payload[:, 12, :9].astype(jnp.int32)
    near_table = permute(own_table, TRANSPOSE)
    tables = (own_table, near_table, jnp.stack([xh, y, core]))

    columns = pl.pallas_call(
        column_kernel,
        out_shape=pltpu.VMEM((8, SLOTS, BS, 128), jnp.float32),
        in_specs=[SMEM, SMEM, VMEM],
        out_specs=VMEM,
        name="columns",
        compiler_params=grant(8),
    )(tables[2], length_scales, payload)
    mine = pltpu.with_memory_space_constraint(dpsi_grad, pltpu.HBM)
    args = (tables, length_scales, columns, z_near, mine, mate)
    far = products((2,), "halves", *args)
    got_up = permute(far[0], Y_UP)
    got_down = permute(far[1], Y_DOWN)
    sides = products((1, 3), "split", *args)
    up_o, up_w, down_o, down_w = (sides[2 * k : 2 * k + 2] for k in range(4))
    direct_up_o = permute(up_o[1], Y_UP)
    direct_down_o = permute(down_o[0], Y_DOWN)
    (here,) = products((0,), "whole", *args)
    local = gradients(tables, length_scales, columns, z_points, (*far, *sides, here))
    sum_up_o = permute(up_o[0] + got_up[:SLOTS], Y_UP)
    sum_down_o = permute(down_o[1] + got_down[:SLOTS], Y_DOWN)
    direct_up_w = permute(up_w[1], Y_UP)
    direct_down_w = permute(down_w[0], Y_DOWN)
    sum_up_w = permute(up_w[0] + got_up[SLOTS:], Y_UP)
    sum_down_w = permute(down_w[1] + got_down[SLOTS:], Y_DOWN)
    sum_o = combine(here, 0, (sum_up_o, direct_down_o), (direct_up_o, sum_down_o))
    got_x = permute(sum_o, SWAP_XH)
    sum_w = combine(here, SLOTS, (sum_up_w, direct_down_w), (direct_up_w, sum_down_w))
    dk_local = finish(sum_w, got_x, block_count)

    total = local + permute(local, SWAP_CORE)
    total = total + permute(total, SWAP_XH)
    total = (total + permute(total, flip_y(1))) + (permute(total, flip_y(2)) + permute(total, flip_y(3)))
    z_grad = total[:3]
    scale = jnp.pad(jnp.sum(total[3, : 3 * BS].reshape(3, BS), axis=1), (0, 125)).reshape(1, 128)
    scale = (scale + permute(scale, flip_z(1))) + (permute(scale, flip_z(2)) + permute(scale, flip_z(3)))
    scale = scale + permute(scale, SWAP_XL)
    scale_grad = scale[0, :3]
    return dk_local.reshape(1, 1, SLOTS, BS, BS), z_grad, scale_grad


def solution(mesh):
    fine = Mesh(mesh.devices.reshape(SIZES), AXES)

    return jax.shard_map(
        on_device,
        mesh=fine,
        in_specs=(
            P(None, DP),
            P(None, IND),
            P(),
            P(DP, IND),
            P(DP, IND, None),
            P(DP, IND, None),
            P(DP, IND),
        ),
        out_specs=(P(DP, IND, None, None, None), P(None, IND), P()),
        check_vma=False,
    )
```
